32 devices in a mesh: seq: 8 (over y, x, core), head: 4 (over z).
Axes of the slice: x: 2, y: 2, z: 4, core: 2. Of those that a mesh axis runs over, the one named last changes fastest.
Arguments:
- queries: bfloat16 [1280, 64, 128], P(('seq', 'head')), may hold values from -8 to 8
- key_one: bfloat16 [1280, 128], P(('seq', 'head')), may hold values from -6 to 6
- value_one: bfloat16 [1280, 128], P(('seq', 'head')), may hold values from -6 to 6
- key_two: bfloat16 [1280, 128], P(('seq', 'head')), may hold values from -6 to 6
- value_two: bfloat16 [1280, 128], P(('seq', 'head')), may hold values from -6 to 6
Outputs:
- attended: bfloat16 [1280, 64, 128], P(('seq', 'head'))
The draws below stay inside these ranges and needn't reach their ends.
All inputs are finite; a program needn't handle non-finite values.
Results may differ from the reference program's by a relative error of at most 0.0058.
Values may be sent and summed in bfloat16 or wider, within the bound.
A program may use at most 64 MiB of HBM per device.

```python
import math
import jax
import jax.numpy as jnp
from jax import lax

HEADS = 64
HEAD_DIM = 128
WIN_ONE = 512
WIN_TWO = 32
SEQ_LEN = 1280


def base_rows(key, shape):
    return jnp.clip(jax.random.normal(key, shape, jnp.float32), -6.0, 6.0)


def draw_key_one(key, part):
    key_rows = base_rows(jax.random.fold_in(key, 11), (SEQ_LEN, HEAD_DIM))
    return key_rows.astype(jnp.bfloat16)


def draw_key_two(key, part):
    key_rows = base_rows(jax.random.fold_in(key, 13), (SEQ_LEN, HEAD_DIM))
    return key_rows.astype(jnp.bfloat16)


def draw_queries(key, part):
    query_rows = base_rows(jax.random.fold_in(key, 17), (SEQ_LEN, HEADS, HEAD_DIM))
    return query_rows.astype(jnp.bfloat16)


def block_scale(stream_key, dims, split, low, high):
    def one(dim, shards_of):
        steps = jax.random.uniform(jax.random.fold_in(jax.random.fold_in(stream_key, 6), dim), (shards_of,), jnp.float32, low / len(split), high / len(split))
        return jnp.repeat(jnp.exp(steps), dims[dim] // shards_of).reshape((-1,) + (1,) * (len(dims) - dim - 1))

    gain = one(*split[0])
    for cut in split[1:]:
        gain = gain * one(*cut)
    return gain


def normal_values(rng, shape, spread, most, cuts=(), kind=jnp.bfloat16):
    gain = block_scale(rng, shape, cuts, -0.22, 0.18) if cuts else 1.0
    drawn = jax.random.normal(rng, shape, jnp.float32) * spread * gain
    return jnp.minimum(jnp.maximum(drawn, -most), most).astype(kind)


def setup_inputs(seed: int = 0) -> dict:
    arg_keys = jax.random.split(jax.random.key(seed), 6)
    return {
        "queries": draw_queries(jax.random.fold_in(arg_keys[5], 71), 0),
        "key_one": draw_key_one(jax.random.fold_in(arg_keys[5], 71), 0),
        "value_one": normal_values(arg_keys[2], (SEQ_LEN, HEAD_DIM), 1.0, 6.0, ((0, 32),)),
        "key_two": draw_key_two(jax.random.fold_in(arg_keys[5], 71), 0),
        "value_two": normal_values(arg_keys[4], (SEQ_LEN, HEAD_DIM), 1.0, 6.0, ((0, 32),)),
    }


def window_attend(query_rows, keys_one, values_one, keys_two, values_two, first_pos):
    block_rows, group_size, head_depth = query_rows.shape
    width_two = keys_two.shape[0] - block_rows + 1
    width_one = keys_one.shape[0] - block_rows + 1
    key_span = keys_one.shape[0]
    near_keys = jnp.stack([keys_two[width_two - 1 - offset:width_two - 1 - offset + block_rows] for offset in range(width_two)], axis=1)
    near_values = jnp.stack([values_two[width_two - 1 - offset:width_two - 1 - offset + block_rows] for offset in range(width_two)], axis=1)
    score_scale = 1.0 / math.sqrt(head_depth)
    product = (query_rows.astype(jnp.float32)[:, :, None, :] * near_keys.astype(jnp.float32)[:, None, :, :] * score_scale).astype(jnp.bfloat16)
    logits = lax.dot_general(product.reshape(-1, head_depth), keys_one, (((1,), (1,)), ((), ())), preferred_element_type=jnp.float32)
    logits = logits.reshape(block_rows, group_size, width_two, key_span)
    row_pos = lax.broadcasted_iota(jnp.int32, (block_rows, 1, 1, 1), 0)
    lag_pos = lax.broadcasted_iota(jnp.int32, (1, 1, width_two, 1), 2)
    col_pos = lax.broadcasted_iota(jnp.int32, (1, 1, 1, key_span), 3)
    inside = (col_pos >= row_pos) & (col_pos <= row_pos + width_one - 1)
    inside = inside & (first_pos - width_one + 1 + col_pos >= 0) & (first_pos + row_pos - lag_pos >= 0)
    logits = jnp.where(inside, logits, -1e+30)
    peak_value = lax.optimization_barrier(jnp.max(logits, axis=(2, 3), keepdims=True))
    raised = jnp.exp(logits - peak_value)
    weights = (raised / lax.optimization_barrier(jnp.sum(raised, axis=(2, 3), keepdims=True))).astype(jnp.bfloat16)
    blended = jnp.dot(weights.reshape(-1, key_span), values_one, preferred_element_type=jnp.float32)
    blended = blended.reshape(block_rows, group_size, width_two, head_depth)
    return lax.optimization_barrier(jnp.sum(blended * near_values.astype(jnp.float32)[:, None, :, :], axis=2))

def reference(queries, key_one, value_one, key_two, value_two):
    total_rows, head_count, head_depth = queries.shape
    block_rows = math.gcd(total_rows, 16)
    zeros_one = jnp.zeros((WIN_ONE - 1, head_depth), key_one.dtype)
    zeros_two = jnp.zeros((WIN_TWO - 1, head_depth), key_two.dtype)
    long_keys_one = jnp.concatenate([zeros_one, key_one], axis=0)
    long_values_one = jnp.concatenate([zeros_one, value_one], axis=0)
    long_keys_two = jnp.concatenate([zeros_two, key_two], axis=0)
    long_values_two = jnp.concatenate([zeros_two, value_two], axis=0)

    def attend(index):
        start = (index * block_rows).astype(jnp.int32)
        query_rows = lax.dynamic_slice_in_dim(queries, start, block_rows, 0)
        keys_one = lax.dynamic_slice_in_dim(long_keys_one, start, block_rows + WIN_ONE - 1, 0)
        values_one = lax.dynamic_slice_in_dim(long_values_one, start, block_rows + WIN_ONE - 1, 0)
        keys_two = lax.dynamic_slice_in_dim(long_keys_two, start, block_rows + WIN_TWO - 1, 0)
        values_two = lax.dynamic_slice_in_dim(long_values_two, start, block_rows + WIN_TWO - 1, 0)
        return window_attend(query_rows, keys_one, values_one, keys_two, values_two, start).astype(jnp.bfloat16)
    blocks = lax.map(attend, jnp.arange(total_rows // block_rows, dtype=jnp.int32))
    return blocks.reshape(total_rows, head_count, head_depth)
```

```python
import functools
import math

import jax
import jax.numpy as jnp
from jax import lax
from jax.experimental import pallas as pl
from jax.experimental.pallas import tpu as pltpu
from jax.sharding import PartitionSpec as P

WIN_ONE = 512
WIN_TWO = 32
LAG_CHUNK = 8


def pieces_behind(window, rows):
    return (window - 2) // rows + 1


def halo_kernel(reach, k1, v1, k2, v2, k1_out, v1_out, k2_out, v2_out, send, recv):
    inner = lax.axis_size("head")
    count = lax.axis_size("seq") * inner
    me = lax.axis_index("seq") * inner + lax.axis_index("head")
    flows = [(k1, k1_out, reach[0]), (v1, v1_out, reach[0])]
    flows += [(k2, k2_out, reach[1]), (v2, v2_out, reach[1])]
    far = max(reach)

    def place(index):
        return (index // inner, index % inner)

    barrier = pltpu.get_barrier_semaphore()
    for step in range(1, far + 1):

        @pl.when(me - step >= 0)
        def _():
            pl.semaphore_signal(
                barrier, inc=1, device_id=place(me - step), device_id_type=pl.DeviceIdType.MESH
            )

    @pl.when(me + 1 < count)
    def _():
        pl.semaphore_wait(barrier, jnp.minimum(far, count - 1 - me))

    def copies(step):
        made = []
        for flow, (source, target, width) in enumerate(flows):
            if step <= width:
                made.append(
                    pltpu.make_async_remote_copy(
                        src_ref=source,
                        dst_ref=target.at[width - step],
                        send_sem=send.at[flow, step - 1],
                        recv_sem=recv.at[flow, step - 1],
                        device_id=place(me + step),
                        device_id_type=pl.DeviceIdType.MESH,
                    )
                )
        return made

    for step in range(far, 0, -1):

        @pl.when(me + step < count)
        def _():
            for copy in copies(step):
                copy.start()

    for step in range(far, 0, -1):

        @pl.when(me + step < count)
        def _():
            for copy in copies(step):
                copy.wait_send()

        @pl.when(me - step >= 0)
        def _():
            for copy in copies(step):
                copy.wait_recv()


def attend_kernel(
    q, k1h, v1h, k2h, v2h, k1, v1, k2, v2, out, k1f, v1f, k2f, v2f, one2, kw, vw, s_first
):
    piece, heads, depth = q.shape
    inner = lax.axis_size("head")
    me = lax.axis_index("seq") * inner + lax.axis_index("head")
    lead_one = k1h.shape[0] * piece
    lead_two = k2h.shape[0] * piece
    scale = 1.0 / math.sqrt(depth)

    def spread(target, behind, own):
        for slot in range(behind.shape[0]):
            target[slot * piece : (slot + 1) * piece, :] = behind[slot].astype(jnp.float32)
        lead = behind.shape[0] * piece
        target[lead : lead + piece, :] = own[...].astype(jnp.float32)

    spread(k1f, k1h, k1)
    spread(v1f, v1h, v1)
    spread(k2f, k2h, k2)
    spread(v2f, v2h, v2)
    first_one = lead_one - me * piece
    first_two = lead_two - me * piece

    @pl.when(first_one > 0)
    def _():
        pos = lax.broadcasted_iota(jnp.int32, k1f.shape, 0)
        whole = k1f[...]
        head_row = jnp.sum(jnp.where(pos == first_one, whole, 0.0), axis=0, keepdims=True)
        k1f[...] = jnp.where(pos < first_one, head_row, whole)
        v1f[...] = jnp.where(pos < first_one, 0.0, v1f[...])

    pos_two = lax.broadcasted_iota(jnp.int32, k2f.shape, 0)
    whole_two = k2f[...]
    head_two = jnp.sum(jnp.where(pos_two == first_two, whole_two, 0.0), axis=0, keepdims=True)
    k2f[...] = jnp.where(pos_two < first_two, head_two, whole_two) * scale
    v2f[...] = jnp.where(pos_two < first_two, 0.0, v2f[...])
    one2[...] = jnp.where(pos_two < first_two, 0.0, 1.0)

    def load_keys(token):
        kw[...] = k1f[pl.ds(lead_one + token - (WIN_ONE - 1), WIN_ONE), :].astype(jnp.bfloat16)

    def logits(token, chunk):
        query = q[token].astype(jnp.float32)
        rows = []
        for lag in range(chunk * LAG_CHUNK, (chunk + 1) * LAG_CHUNK):
            near = k2f[pl.ds(lead_two + token - lag, 1), :]
            rows.append((query * near).astype(jnp.bfloat16))
        return lax.dot_general(
            jnp.concatenate(rows, axis=0),
            kw[...],
            (((1,), (1,)), ((), ())),
            preferred_element_type=jnp.float32,
        )

    load_keys(0)
    s_first[...] = logits(0, 0)
    lane_pos = lax.broadcasted_iota(jnp.int32, (WIN_ONE, depth), 0)

    def step(token, carry):
        start = lead_one + token - (WIN_ONE - 1)
        vw[:, :depth] = v1f[pl.ds(start, WIN_ONE), :].astype(jnp.bfloat16)
        vw[:, depth:] = jnp.where(lane_pos + start < first_one, 0.0, 1.0).astype(jnp.bfloat16)
        peak = num = den = None
        chunks = WIN_TWO // LAG_CHUNK
        scores = s_first[...]
        for chunk in range(chunks):
            if chunk + 1 < chunks:
                following = logits(token, chunk + 1)
            else:
                later = jnp.minimum(token + 1, piece - 1)
                load_keys(later)
                s_first[...] = logits(later, 0)
            parts = scores.reshape(LAG_CHUNK, heads, WIN_ONE)
            top = jnp.max(jnp.max(parts, axis=0), axis=1, keepdims=True)
            raised_peak = top if peak is None else jnp.maximum(peak, top)
            raised = jnp.exp(parts - raised_peak[None]).astype(jnp.bfloat16)
            mixed = jnp.dot(
                raised.reshape(LAG_CHUNK * heads, WIN_ONE), vw[...], preferred_element_type=jnp.float32
            )
            mixed = mixed.reshape(LAG_CHUNK, heads, 2 * depth)
            if peak is not None:
                fade = jnp.exp(peak - raised_peak)
                num = num * fade
                den = den * fade
            for index in range(LAG_CHUNK):
                row = lead_two + token - (chunk * LAG_CHUNK + index)
                more = mixed[index, :, :depth] * v2f[pl.ds(row, 1), :]
                count = mixed[index, :, depth:] * one2[pl.ds(row, 1), :]
                num = more if num is None else num + more
                den = count if den is None else den + count
            peak = raised_peak
            if chunk + 1 < chunks:
                scores = following
        out[token] = (num / den).astype(out.dtype)
        return carry

    lax.fori_loop(0, piece, step, 0)


def body(queries, key_one, value_one, key_two, value_two):
    piece, heads, depth = queries.shape
    reach = (pieces_behind(WIN_ONE, piece), pieces_behind(WIN_TWO, piece))
    anywhere = pl.BlockSpec(memory_space=pl.ANY)
    vmem = pl.BlockSpec(memory_space=pltpu.VMEM)
    behind = [jax.ShapeDtypeStruct((r, piece, depth), key_one.dtype) for r in (reach[0], reach[0], reach[1], reach[1])]
    halos = pl.pallas_call(
        functools.partial(halo_kernel, reach),
        out_shape=behind,
        in_specs=[anywhere] * 4,
        out_specs=[anywhere] * 4,
        scratch_shapes=[
            pltpu.SemaphoreType.DMA((4, max(reach))),
            pltpu.SemaphoreType.DMA((4, max(reach))),
        ],
        compiler_params=pltpu.CompilerParams(collective_id=0, has_side_effects=True),
    )(key_one, value_one, key_two, value_two)
    long_one = ((reach[0] + 1) * piece, depth)
    long_two = ((reach[1] + 1) * piece, depth)
    return pl.pallas_call(
        attend_kernel,
        out_shape=jax.ShapeDtypeStruct(queries.shape, queries.dtype),
        in_specs=[vmem] * 9,
        out_specs=vmem,
        scratch_shapes=[
            pltpu.VMEM(long_one, jnp.float32),
            pltpu.VMEM(long_one, jnp.float32),
            pltpu.VMEM(long_two, jnp.float32),
            pltpu.VMEM(long_two, jnp.float32),
            pltpu.VMEM(long_two, jnp.float32),
            pltpu.VMEM((WIN_ONE, depth), jnp.bfloat16),
            pltpu.VMEM((WIN_ONE, 2 * depth), jnp.bfloat16),
            pltpu.VMEM((LAG_CHUNK * heads, WIN_ONE), jnp.float32),
        ],
        compiler_params=pltpu.CompilerParams(vmem_limit_bytes=48 * 1024 * 1024),
    )(queries, *halos, key_one, value_one, key_two, value_two)


def solution(mesh):
    rows = P(("seq", "head"), None)
    placed = (P(("seq", "head"), None, None), rows, rows, rows, rows)
    return jax.shard_map(
        body, mesh=mesh, in_specs=placed, out_specs=P(("seq", "head"), None, None), check_vma=False
    )
```

```python
import functools
import math

import jax
import jax.numpy as jnp
from jax import lax
from jax.experimental import pallas as pl
from jax.experimental.pallas import tpu as pltpu
from jax.sharding import PartitionSpec as P

WIN_ONE = 512
WIN_TWO = 32
LAG_CHUNK = 8
ROW_L = 1
COL_L = 2
ROW_B = 2


def pieces_behind(window, rows):
    return (window - 2) // rows + 1


def halo_kernel(reach, k1, v1, k2, v2, k1_out, v1_out, k2_out, v2_out, send, recv):
    inner = lax.axis_size("head")
    count = lax.axis_size("seq") * inner
    me = lax.axis_index("seq") * inner + lax.axis_index("head")
    flows = [(k1, k1_out, reach[0]), (v1, v1_out, reach[0])]
    flows += [(k2, k2_out, reach[1]), (v2, v2_out, reach[1])]
    far = max(reach)

    def place(index):
        return (index // inner, index % inner)

    barrier = pltpu.get_barrier_semaphore()
    for step in range(1, far + 1):

        @pl.when(me - step >= 0)
        def _():
            pl.semaphore_signal(
                barrier, inc=1, device_id=place(me - step), device_id_type=pl.DeviceIdType.MESH
            )

    @pl.when(me + 1 < count)
    def _():
        pl.semaphore_wait(barrier, jnp.minimum(far, count - 1 - me))

    def copies(step):
        made = []
        for flow, (source, target, width) in enumerate(flows):
            if step <= width:
                made.append(
                    pltpu.make_async_remote_copy(
                        src_ref=source,
                        dst_ref=target.at[width - step],
                        send_sem=send.at[flow, step - 1],
                        recv_sem=recv.at[flow, step - 1],
                        device_id=place(me + step),
                        device_id_type=pl.DeviceIdType.MESH,
                    )
                )
        return made

    for step in range(far, 0, -1):

        @pl.when(me + step < count)
        def _():
            for copy in copies(step):
                copy.start()

    for step in range(far, 0, -1):

        @pl.when(me + step < count)
        def _():
            for copy in copies(step):
                copy.wait_send()

        @pl.when(me - step >= 0)
        def _():
            for copy in copies(step):
                copy.wait_recv()


def attend_kernel(
    q, k1h, v1h, k2h, v2h, k1, v1, k2, v2, out, k1f, v1f, k2f, v2f, one2, kw, vw, scores
):
    piece, heads, depth = q.shape
    inner = lax.axis_size("head")
    me = lax.axis_index("seq") * inner + lax.axis_index("head")
    lead_one = k1h.shape[0] * piece
    lead_two = k2h.shape[0] * piece
    scale = 1.0 / math.sqrt(depth)

    def spread(target, behind, own):
        for slot in range(behind.shape[0]):
            target[slot * piece : (slot + 1) * piece, :] = behind[slot].astype(jnp.float32)
        lead = behind.shape[0] * piece
        target[lead : lead + piece, :] = own[...].astype(jnp.float32)

    spread(k1f, k1h, k1)
    spread(v1f, v1h, v1)
    spread(k2f, k2h, k2)
    spread(v2f, v2h, v2)
    first_one = lead_one - me * piece
    first_two = lead_two - me * piece

    @pl.when(first_one > 0)
    def _():
        pos = lax.broadcasted_iota(jnp.int32, k1f.shape, 0)
        whole = k1f[...]
        head_row = jnp.sum(jnp.where(pos == first_one, whole, 0.0), axis=0, keepdims=True)
        k1f[...] = jnp.where(pos < first_one, head_row, whole)
        v1f[...] = jnp.where(pos < first_one, 0.0, v1f[...])

    pos_two = lax.broadcasted_iota(jnp.int32, k2f.shape, 0)
    whole_two = k2f[...]
    head_two = jnp.sum(jnp.where(pos_two == first_two, whole_two, 0.0), axis=0, keepdims=True)
    k2f[...] = jnp.where(pos_two < first_two, head_two, whole_two) * scale
    v2f[...] = jnp.where(pos_two < first_two, 0.0, v2f[...])
    one2[...] = jnp.where(pos_two < first_two, 0.0, 1.0)

    span = LAG_CHUNK * heads
    lane_pos = lax.broadcasted_iota(jnp.int32, (WIN_ONE, depth), 0)

    def load_keys(token):
        kw[...] = k1f[pl.ds(lead_one + token - (WIN_ONE - 1), WIN_ONE), :].astype(jnp.bfloat16)

    def logits(token, chunk, top):
        query = q[token].astype(jnp.float32)
        rows = []
        for lag in range(chunk * LAG_CHUNK, (chunk + 1) * LAG_CHUNK):
            near = k2f[pl.ds(lead_two + token - lag, 1), :]
            rows.append((query * near).astype(jnp.bfloat16))
        product = jnp.concatenate(rows, axis=0)
        for lo in range(0, span, span // ROW_L):
            for col in range(0, WIN_ONE, WIN_ONE // COL_L):
                made = lax.dot_general(
                    product[lo : lo + span // ROW_L],
                    kw[col : col + WIN_ONE // COL_L, :],
                    (((1,), (1,)), ((), ())),
                    preferred_element_type=jnp.float32,
                )
                scores[chunk * span + lo : chunk * span + lo + span // ROW_L, col : col + WIN_ONE // COL_L] = made
                best = jnp.max(made.reshape(LAG_CHUNK // ROW_L, heads, WIN_ONE // COL_L), axis=0)
                for lane in range(0, WIN_ONE // COL_L, depth):
                    part = best[:, lane : lane + depth]
                    top = part if top is None else jnp.maximum(top, part)
        return top

    chunks = WIN_TWO // LAG_CHUNK
    load_keys(0)
    start_top = None
    for chunk in range(chunks):
        start_top = logits(0, chunk, start_top)

    def step(token, top):
        start = lead_one + token - (WIN_ONE - 1)
        vw[:, :depth] = v1f[pl.ds(start, WIN_ONE), :].astype(jnp.bfloat16)
        vw[:, depth:] = jnp.where(lane_pos + start < first_one, 0.0, 1.0).astype(jnp.bfloat16)
        later = jnp.minimum(token + 1, piece - 1)
        load_keys(later)
        peak = jnp.max(top, axis=1, keepdims=True)
        num = den = later_top = None
        for chunk in range(chunks):
            sub = LAG_CHUNK // ROW_B
            for lo in range(0, LAG_CHUNK, sub):
                base = (chunk * LAG_CHUNK + lo) * heads
                parts = scores[base : base + sub * heads, :].reshape(sub, heads, WIN_ONE)
                raised = jnp.exp(parts - peak[None]).astype(jnp.bfloat16)
                mixed = jnp.dot(
                    raised.reshape(sub * heads, WIN_ONE), vw[...], preferred_element_type=jnp.float32
                )
                mixed = mixed.reshape(sub, heads, 2 * depth)
                for index in range(sub):
                    row = lead_two + token - (chunk * LAG_CHUNK + lo + index)
                    more = mixed[index, :, :depth] * v2f[pl.ds(row, 1), :]
                    count = mixed[index, :, depth:] * one2[pl.ds(row, 1), :]
                    num = more if num is None else num + more
                    den = count if den is None else den + count
            later_top = logits(later, chunk, later_top)
        out[token] = (num / den).astype(out.dtype)
        return later_top

    lax.fori_loop(0, piece, step, start_top)


def body(queries, key_one, value_one, key_two, value_two):
    piece, heads, depth = queries.shape
    reach = (pieces_behind(WIN_ONE, piece), pieces_behind(WIN_TWO, piece))
    anywhere = pl.BlockSpec(memory_space=pl.ANY)
    vmem = pl.BlockSpec(memory_space=pltpu.VMEM)
    behind = [jax.ShapeDtypeStruct((r, piece, depth), key_one.dtype) for r in (reach[0], reach[0], reach[1], reach[1])]
    halos = pl.pallas_call(
        functools.partial(halo_kernel, reach),
        out_shape=behind,
        in_specs=[anywhere] * 4,
        out_specs=[anywhere] * 4,
        scratch_shapes=[
            pltpu.SemaphoreType.DMA((4, max(reach))),
            pltpu.SemaphoreType.DMA((4, max(reach))),
        ],
        compiler_params=pltpu.CompilerParams(collective_id=0, has_side_effects=True),
    )(key_one, value_one, key_two, value_two)
    long_one = ((reach[0] + 1) * piece, depth)
    long_two = ((reach[1] + 1) * piece, depth)
    return pl.pallas_call(
        attend_kernel,
        out_shape=jax.ShapeDtypeStruct(queries.shape, queries.dtype),
        in_specs=[vmem] * 9,
        out_specs=vmem,
        scratch_shapes=[
            pltpu.VMEM(long_one, jnp.float32),
            pltpu.VMEM(long_one, jnp.float32),
            pltpu.VMEM(long_two, jnp.float32),
            pltpu.VMEM(long_two, jnp.float32),
            pltpu.VMEM(long_two, jnp.float32),
            pltpu.VMEM((WIN_ONE, depth), jnp.bfloat16),
            pltpu.VMEM((WIN_ONE, 2 * depth), jnp.bfloat16),
            pltpu.VMEM((WIN_TWO * heads, WIN_ONE), jnp.float32),
        ],
        compiler_params=pltpu.CompilerParams(vmem_limit_bytes=48 * 1024 * 1024),
    )(queries, *halos, key_one, value_one, key_two, value_two)


def solution(mesh):
    rows = P(("seq", "head"), None)
    placed = (P(("seq", "head"), None, None), rows, rows, rows, rows)
    return jax.shard_map(
        body, mesh=mesh, in_specs=placed, out_specs=P(("seq", "head"), None, None), check_vma=False
    )
```

```python
import functools
import math

import jax
import jax.numpy as jnp
from jax import lax
from jax.experimental import pallas as pl
from jax.experimental.pallas import tpu as pltpu
from jax.sharding import PartitionSpec as P

WIN_ONE = 512
WIN_TWO = 32
LAG_CHUNK = 8
ROW_L = 1
COL_L = 2
ROW_B = 4


def pieces_behind(window, rows):
    return (window - 2) // rows + 1


def halo_kernel(reach, k1, v1, k2, v2, k1_out, v1_out, k2_out, v2_out, send, recv):
    inner = lax.axis_size("head")
    count = lax.axis_size("seq") * inner
    me = lax.axis_index("seq") * inner + lax.axis_index("head")
    flows = [(k1, k1_out, reach[0]), (v1, v1_out, reach[0])]
    flows += [(k2, k2_out, reach[1]), (v2, v2_out, reach[1])]
    far = max(reach)

    def place(index):
        return (index // inner, index % inner)

    barrier = pltpu.get_barrier_semaphore()
    for step in range(1, far + 1):

        @pl.when(me - step >= 0)
        def _():
            pl.semaphore_signal(
                barrier, inc=1, device_id=place(me - step), device_id_type=pl.DeviceIdType.MESH
            )

    @pl.when(me + 1 < count)
    def _():
        pl.semaphore_wait(barrier, jnp.minimum(far, count - 1 - me))

    def copies(step):
        made = []
        for flow, (source, target, width) in enumerate(flows):
            if step <= width:
                made.append(
                    pltpu.make_async_remote_copy(
                        src_ref=source,
                        dst_ref=target.at[width - step],
                        send_sem=send.at[flow, step - 1],
                        recv_sem=recv.at[flow, step - 1],
                        device_id=place(me + step),
                        device_id_type=pl.DeviceIdType.MESH,
                    )
                )
        return made

    for step in range(far, 0, -1):

        @pl.when(me + step < count)
        def _():
            for copy in copies(step):
                copy.start()

    for step in range(far, 0, -1):

        @pl.when(me + step < count)
        def _():
            for copy in copies(step):
                copy.wait_send()

        @pl.when(me - step >= 0)
        def _():
            for copy in copies(step):
                copy.wait_recv()


def attend_kernel(*refs):
    q_far, far, out, q, near, fetched = refs[0], refs[1:9], refs[9], refs[10], refs[11:19], refs[19]
    k1f, v1f, k2f, v2f, one2, kw, vw, scores = refs[20:]
    piece, heads, depth = q.shape
    fetches = [
        pltpu.make_async_copy(source, target, fetched.at[index])
        for index, (source, target) in enumerate(zip(far, near))
    ]
    early = pltpu.make_async_copy(q_far.at[pl.ds(0, 1)], q.at[pl.ds(0, 1)], fetched.at[8])
    rest = pltpu.make_async_copy(q_far.at[pl.ds(1, piece - 1)], q.at[pl.ds(1, piece - 1)], fetched.at[9])
    for fetch in fetches:
        fetch.start()
    early.start()
    rest.start()
    k1h, v1h, k2h, v2h, k1, v1, k2, v2 = near
    for fetch in fetches:
        fetch.wait()
    inner = lax.axis_size("head")
    me = lax.axis_index("seq") * inner + lax.axis_index("head")
    lead_one = k1h.shape[0] * piece
    lead_two = k2h.shape[0] * piece
    scale = 1.0 / math.sqrt(depth)

    def spread(target, behind, own):
        for slot in range(behind.shape[0]):
            target[slot * piece : (slot + 1) * piece, :] = behind[slot].astype(jnp.float32)
        lead = behind.shape[0] * piece
        target[lead : lead + piece, :] = own[...].astype(jnp.float32)

    spread(k1f, k1h, k1)
    spread(v1f, v1h, v1)
    spread(k2f, k2h, k2)
    spread(v2f, v2h, v2)
    first_one = lead_one - me * piece
    first_two = lead_two - me * piece

    @pl.when(first_one > 0)
    def _():
        pos = lax.broadcasted_iota(jnp.int32, k1f.shape, 0)
        whole = k1f[...]
        head_row = jnp.sum(jnp.where(pos == first_one, whole, 0.0), axis=0, keepdims=True)
        k1f[...] = jnp.where(pos < first_one, head_row, whole)
        v1f[...] = jnp.where(pos < first_one, 0.0, v1f[...])

    pos_two = lax.broadcasted_iota(jnp.int32, k2f.shape, 0)
    whole_two = k2f[...]
    head_two = jnp.sum(jnp.where(pos_two == first_two, whole_two, 0.0), axis=0, keepdims=True)
    k2f[...] = jnp.where(pos_two < first_two, head_two, whole_two) * scale
    v2f[...] = jnp.where(pos_two < first_two, 0.0, v2f[...])
    one2[...] = jnp.where(pos_two < first_two, 0.0, 1.0)

    span = LAG_CHUNK * heads
    lane_pos = lax.broadcasted_iota(jnp.int32, (WIN_ONE, depth), 0)

    def load_keys(token):
        kw[...] = k1f[pl.ds(lead_one + token - (WIN_ONE - 1), WIN_ONE), :].astype(jnp.bfloat16)

    def logits(token, chunk, top):
        query = q[token].astype(jnp.float32)
        rows = []
        for lag in range(chunk * LAG_CHUNK, (chunk + 1) * LAG_CHUNK):
            near = k2f[pl.ds(lead_two + token - lag, 1), :]
            rows.append((query * near).astype(jnp.bfloat16))
        product = jnp.concatenate(rows, axis=0)
        for lo in range(0, span, span // ROW_L):
            for col in range(0, WIN_ONE, WIN_ONE // COL_L):
                made = lax.dot_general(
                    product[lo : lo + span // ROW_L],
                    kw[col : col + WIN_ONE // COL_L, :],
                    (((1,), (1,)), ((), ())),
                    preferred_element_type=jnp.float32,
                )
                scores[chunk * span + lo : chunk * span + lo + span // ROW_L, col : col + WIN_ONE // COL_L] = made
                best = jnp.max(made.reshape(LAG_CHUNK // ROW_L, heads, WIN_ONE // COL_L), axis=0)
                for lane in range(0, WIN_ONE // COL_L, depth):
                    part = best[:, lane : lane + depth]
                    top = part if top is None else jnp.maximum(top, part)
        return top

    chunks = WIN_TWO // LAG_CHUNK
    load_keys(0)
    early.wait()
    start_top = None
    for chunk in range(chunks):
        start_top = logits(0, chunk, start_top)

    def step(token, top):
        start = lead_one + token - (WIN_ONE - 1)
        vw[:, :depth] = v1f[pl.ds(start, WIN_ONE), :].astype(jnp.bfloat16)
        vw[:, depth:] = jnp.where(lane_pos + start < first_one, 0.0, 1.0).astype(jnp.bfloat16)
        later = jnp.minimum(token + 1, piece - 1)
        load_keys(later)
        peak = jnp.max(top, axis=1, keepdims=True)
        num = den = later_top = None
        for chunk in range(chunks):
            sub = LAG_CHUNK // ROW_B
            for lo in range(0, LAG_CHUNK, sub):
                base = (chunk * LAG_CHUNK + lo) * heads
                parts = scores[base : base + sub * heads, :].reshape(sub, heads, WIN_ONE)
                raised = jnp.exp(parts - peak[None]).astype(jnp.bfloat16)
                mixed = jnp.dot(
                    raised.reshape(sub * heads, WIN_ONE), vw[...], preferred_element_type=jnp.float32
                )
                mixed = mixed.reshape(sub, heads, 2 * depth)
                for index in range(sub):
                    row = lead_two + token - (chunk * LAG_CHUNK + lo + index)
                    more = mixed[index, :, :depth] * v2f[pl.ds(row, 1), :]
                    count = mixed[index, :, depth:] * one2[pl.ds(row, 1), :]
                    num = more if num is None else num + more
                    den = count if den is None else den + count
            later_top = logits(later, chunk, later_top)
        out[token] = (num / den).astype(out.dtype)
        return later_top

    rest.wait()
    lax.fori_loop(0, piece, step, start_top)


def body(queries, key_one, value_one, key_two, value_two):
    piece, heads, depth = queries.shape
    reach = (pieces_behind(WIN_ONE, piece), pieces_behind(WIN_TWO, piece))
    anywhere = pl.BlockSpec(memory_space=pl.ANY)
    vmem = pl.BlockSpec(memory_space=pltpu.VMEM)
    behind = [jax.ShapeDtypeStruct((r, piece, depth), key_one.dtype) for r in (reach[0], reach[0], reach[1], reach[1])]
    halos = pl.pallas_call(
        functools.partial(halo_kernel, reach),
        out_shape=behind,
        in_specs=[anywhere] * 4,
        out_specs=[anywhere] * 4,
        scratch_shapes=[
            pltpu.SemaphoreType.DMA((4, max(reach))),
            pltpu.SemaphoreType.DMA((4, max(reach))),
        ],
        compiler_params=pltpu.CompilerParams(collective_id=0, has_side_effects=True),
    )(key_one, value_one, key_two, value_two)
    long_one = ((reach[0] + 1) * piece, depth)
    long_two = ((reach[1] + 1) * piece, depth)
    return pl.pallas_call(
        attend_kernel,
        out_shape=jax.ShapeDtypeStruct(queries.shape, queries.dtype),
        in_specs=[anywhere] * 9,
        out_specs=vmem,
        scratch_shapes=[
            pltpu.VMEM(queries.shape, queries.dtype),
            *[pltpu.VMEM(x.shape, x.dtype) for x in (*halos, key_one, value_one, key_two, value_two)],
            pltpu.SemaphoreType.DMA((10,)),
            pltpu.VMEM(long_one, jnp.float32),
            pltpu.VMEM(long_one, jnp.float32),
            pltpu.VMEM(long_two, jnp.float32),
            pltpu.VMEM(long_two, jnp.float32),
            pltpu.VMEM(long_two, jnp.float32),
            pltpu.VMEM((WIN_ONE, depth), jnp.bfloat16),
            pltpu.VMEM((WIN_ONE, 2 * depth), jnp.bfloat16),
            pltpu.VMEM((WIN_TWO * heads, WIN_ONE), jnp.float32),
        ],
    )(queries, *halos, key_one, value_one, key_two, value_two)


def solution(mesh):
    rows = P(("seq", "head"), None)
    placed = (P(("seq", "head"), None, None), rows, rows, rows, rows)
    return jax.shard_map(
        body, mesh=mesh, in_specs=placed, out_specs=P(("seq", "head"), None, None), check_vma=False
    )
```

```python
import functools
import math

import jax
import jax.numpy as jnp
from jax import lax
from jax.experimental import pallas as pl
from jax.experimental.pallas import tpu as pltpu
from jax.sharding import PartitionSpec as P

WIN_ONE = 512
WIN_TWO = 32
LAG_CHUNK = 8
ROW_L = 1
COL_L = 2
ROW_B = 4


def pieces_behind(window, rows):
    return (window - 2) // rows + 1


def shards_behind(reach, inner):
    return (reach + inner - 1) // inner


def halo_kernel(reach, k1, v1, k2, v2, k1_out, v1_out, k2_out, v2_out, *sems):
    side_send, side_recv, fore_send, fore_recv, near_send, near_recv = sems
    inner, outer = lax.axis_size("head"), lax.axis_size("seq")
    seq, col = lax.axis_index("seq"), lax.axis_index("head")
    me, count = seq * inner + col, outer * inner
    shards = shards_behind(reach[0], inner)
    base = shards * inner
    firsts = ((k1, k1_out), (v1, v1_out))
    seconds = ((k2, k2_out), (v2, v2_out))

    def remote(source, target, send, recv, where):
        return pltpu.make_async_remote_copy(
            src_ref=source,
            dst_ref=target,
            send_sem=send,
            recv_sem=recv,
            device_id=where,
            device_id_type=pl.DeviceIdType.MESH,
        )

    def around(turn):
        return (col + turn) % inner

    def side(turn):
        return [
            remote(
                source,
                target.at[base + col],
                side_send.at[flow, turn - 1],
                side_recv.at[flow, turn - 1],
                (seq, around(turn)),
            )
            for flow, (source, target) in enumerate(firsts)
        ]

    def side_arrival(turn):
        return [
            remote(
                source,
                target.at[base + around(turn)],
                side_send.at[flow, inner - turn - 1],
                side_recv.at[flow, inner - turn - 1],
                (seq, around(turn)),
            )
            for flow, (source, target) in enumerate(firsts)
        ]

    def fore(hop, turn):
        return [
            remote(
                source if turn == 0 else target.at[base + around(turn)],
                target.at[(shards - hop) * inner + around(turn)],
                fore_send.at[flow, hop - 1, turn],
                fore_recv.at[flow, hop - 1, turn],
                (seq + hop, col),
            )
            for flow, (source, target) in enumerate(firsts)
        ]

    def near(step):
        there = me + step
        return [
            remote(
                source,
                target.at[reach[1] - step],
                near_send.at[flow, step - 1],
                near_recv.at[flow, step - 1],
                (there // inner, there % inner),
            )
            for flow, (source, target) in enumerate(seconds)
        ]

    def wanted(hop, turn):
        return hop * inner <= reach[0] + around(turn) - col

    def greet(where):
        pl.semaphore_signal(barrier, inc=1, device_id=where, device_id_type=pl.DeviceIdType.MESH)

    barrier = pltpu.get_barrier_semaphore()
    hops = (reach[0] + inner - 1 - col) // inner
    for turn in range(1, inner):
        greet((seq, around(turn)))
    for hop in range(1, shards + 1):

        @pl.when((seq - hop >= 0) & (hop <= hops))
        def _():
            greet((seq - hop, col))

    for step in range(1, reach[1] + 1):

        @pl.when(me - step >= 0)
        def _():
            greet(((me - step) // inner, (me - step) % inner))

    peers = inner - 1 + jnp.minimum(hops, outer - 1 - seq) + jnp.minimum(reach[1], count - 1 - me)
    pl.semaphore_wait(barrier, peers)

    for turn in range(1, inner):
        for copy in side(turn):
            copy.start()
    for turn in range(inner):
        if turn:
            for copy in side_arrival(turn):
                copy.wait_recv()
        for hop in range(shards, 0, -1):

            @pl.when((seq + hop < outer) & wanted(hop, turn))
            def _():
                for copy in fore(hop, turn):
                    copy.start()

        if turn == 0:
            for step in range(1, reach[1] + 1):

                @pl.when(me + step < count)
                def _():
                    for copy in near(step):
                        copy.start()

    for turn in range(inner):
        for hop in range(shards, 0, -1):

            @pl.when((seq - hop >= 0) & wanted(hop, turn))
            def _():
                for copy in fore(hop, turn):
                    copy.wait_recv()

            @pl.when((seq + hop < outer) & wanted(hop, turn))
            def _():
                for copy in fore(hop, turn):
                    copy.wait_send()

    for step in range(1, reach[1] + 1):

        @pl.when(me - step >= 0)
        def _():
            for copy in near(step):
                copy.wait_recv()

        @pl.when(me + step < count)
        def _():
            for copy in near(step):
                copy.wait_send()

    for turn in range(1, inner):
        for copy in side(turn):
            copy.wait_send()


def attend_kernel(*refs):
    q_far, far, out, q, near, fetched = refs[0], refs[1:9], refs[9], refs[10], refs[11:19], refs[19]
    k1f, v1f, k2f, v2f, one2, kw, vw, scores = refs[20:]
    piece, heads, depth = q.shape
    inner = lax.axis_size("head")
    reach = near[0].shape[0]
    skip = lax.axis_index("head") + shards_behind(reach, inner) * inner - reach
    far = [far[0].at[pl.ds(skip, reach)], far[1].at[pl.ds(skip, reach)], *far[2:]]
    fetches = [
        pltpu.make_async_copy(source, target, fetched.at[index])
        for index, (source, target) in enumerate(zip(far, near))
    ]
    early = pltpu.make_async_copy(q_far.at[pl.ds(0, 1)], q.at[pl.ds(0, 1)], fetched.at[8])
    rest = pltpu.make_async_copy(q_far.at[pl.ds(1, piece - 1)], q.at[pl.ds(1, piece - 1)], fetched.at[9])
    for fetch in fetches:
        fetch.start()
    early.start()
    rest.start()
    k1h, v1h, k2h, v2h, k1, v1, k2, v2 = near
    for fetch in fetches:
        fetch.wait()
    inner = lax.axis_size("head")
    me = lax.axis_index("seq") * inner + lax.axis_index("head")
    lead_one = k1h.shape[0] * piece
    lead_two = k2h.shape[0] * piece
    scale = 1.0 / math.sqrt(depth)

    def spread(target, behind, own):
        for slot in range(behind.shape[0]):
            target[slot * piece : (slot + 1) * piece, :] = behind[slot].astype(jnp.float32)
        lead = behind.shape[0] * piece
        target[lead : lead + piece, :] = own[...].astype(jnp.float32)

    spread(k1f, k1h, k1)
    spread(v1f, v1h, v1)
    spread(k2f, k2h, k2)
    spread(v2f, v2h, v2)
    first_one = lead_one - me * piece
    first_two = lead_two - me * piece

    @pl.when(first_one > 0)
    def _():
        pos = lax.broadcasted_iota(jnp.int32, k1f.shape, 0)
        whole = k1f[...]
        head_row = jnp.sum(jnp.where(pos == first_one, whole, 0.0), axis=0, keepdims=True)
        k1f[...] = jnp.where(pos < first_one, head_row, whole)
        v1f[...] = jnp.where(pos < first_one, 0.0, v1f[...])

    pos_two = lax.broadcasted_iota(jnp.int32, k2f.shape, 0)
    whole_two = k2f[...]
    head_two = jnp.sum(jnp.where(pos_two == first_two, whole_two, 0.0), axis=0, keepdims=True)
    k2f[...] = jnp.where(pos_two < first_two, head_two, whole_two) * scale
    v2f[...] = jnp.where(pos_two < first_two, 0.0, v2f[...])
    one2[...] = jnp.where(pos_two < first_two, 0.0, 1.0)

    span = LAG_CHUNK * heads
    lane_pos = lax.broadcasted_iota(jnp.int32, (WIN_ONE, depth), 0)

    def load_keys(token):
        kw[...] = k1f[pl.ds(lead_one + token - (WIN_ONE - 1), WIN_ONE), :].astype(jnp.bfloat16)

    def logits(token, chunk, top):
        query = q[token].astype(jnp.float32)
        rows = []
        for lag in range(chunk * LAG_CHUNK, (chunk + 1) * LAG_CHUNK):
            near = k2f[pl.ds(lead_two + token - lag, 1), :]
            rows.append((query * near).astype(jnp.bfloat16))
        product = jnp.concatenate(rows, axis=0)
        for lo in range(0, span, span // ROW_L):
            for col in range(0, WIN_ONE, WIN_ONE // COL_L):
                made = lax.dot_general(
                    product[lo : lo + span // ROW_L],
                    kw[col : col + WIN_ONE // COL_L, :],
                    (((1,), (1,)), ((), ())),
                    preferred_element_type=jnp.float32,
                )
                scores[chunk * span + lo : chunk * span + lo + span // ROW_L, col : col + WIN_ONE // COL_L] = made
                best = jnp.max(made.reshape(LAG_CHUNK // ROW_L, heads, WIN_ONE // COL_L), axis=0)
                for lane in range(0, WIN_ONE // COL_L, depth):
                    part = best[:, lane : lane + depth]
                    top = part if top is None else jnp.maximum(top, part)
        return top

    chunks = WIN_TWO // LAG_CHUNK
    load_keys(0)
    early.wait()
    start_top = None
    for chunk in range(chunks):
        start_top = logits(0, chunk, start_top)

    def step(token, top):
        start = lead_one + token - (WIN_ONE - 1)
        vw[:, :depth] = v1f[pl.ds(start, WIN_ONE), :].astype(jnp.bfloat16)
        vw[:, depth:] = jnp.where(lane_pos + start < first_one, 0.0, 1.0).astype(jnp.bfloat16)
        later = jnp.minimum(token + 1, piece - 1)
        load_keys(later)
        peak = jnp.max(top, axis=1, keepdims=True)
        num = den = later_top = None
        for chunk in range(chunks):
            sub = LAG_CHUNK // ROW_B
            for lo in range(0, LAG_CHUNK, sub):
                base = (chunk * LAG_CHUNK + lo) * heads
                parts = scores[base : base + sub * heads, :].reshape(sub, heads, WIN_ONE)
                raised = jnp.exp(parts - peak[None]).astype(jnp.bfloat16)
                mixed = jnp.dot(
                    raised.reshape(sub * heads, WIN_ONE), vw[...], preferred_element_type=jnp.float32
                )
                mixed = mixed.reshape(sub, heads, 2 * depth)
                for index in range(sub):
                    row = lead_two + token - (chunk * LAG_CHUNK + lo + index)
                    more = mixed[index, :, :depth] * v2f[pl.ds(row, 1), :]
                    count = mixed[index, :, depth:] * one2[pl.ds(row, 1), :]
                    num = more if num is None else num + more
                    den = count if den is None else den + count
            later_top = logits(later, chunk, later_top)
        out[token] = (num / den).astype(out.dtype)
        return later_top

    rest.wait()
    lax.fori_loop(0, piece, step, start_top)


def body(queries, key_one, value_one, key_two, value_two):
    piece, heads, depth = queries.shape
    reach = (pieces_behind(WIN_ONE, piece), pieces_behind(WIN_TWO, piece))
    anywhere = pl.BlockSpec(memory_space=pl.ANY)
    vmem = pl.BlockSpec(memory_space=pltpu.VMEM)
    inner = lax.axis_size("head")
    shards = shards_behind(reach[0], inner)
    slots = (shards + 1) * inner
    behind = [jax.ShapeDtypeStruct((r, piece, depth), key_one.dtype) for r in (slots, slots, reach[1], reach[1])]
    windows = [jax.ShapeDtypeStruct((r, piece, depth), key_one.dtype) for r in (reach[0], reach[0], reach[1], reach[1])]
    halos = pl.pallas_call(
        functools.partial(halo_kernel, reach),
        out_shape=behind,
        in_specs=[anywhere] * 4,
        out_specs=[anywhere] * 4,
        scratch_shapes=[
            *[pltpu.SemaphoreType.DMA((2, inner))] * 2,
            *[pltpu.SemaphoreType.DMA((2, shards, inner))] * 2,
            *[pltpu.SemaphoreType.DMA((2, reach[1]))] * 2,
        ],
        compiler_params=pltpu.CompilerParams(collective_id=0, has_side_effects=True),
    )(key_one, value_one, key_two, value_two)
    long_one = ((reach[0] + 1) * piece, depth)
    long_two = ((reach[1] + 1) * piece, depth)
    return pl.pallas_call(
        attend_kernel,
        out_shape=jax.ShapeDtypeStruct(queries.shape, queries.dtype),
        in_specs=[anywhere] * 9,
        out_specs=vmem,
        scratch_shapes=[
            pltpu.VMEM(queries.shape, queries.dtype),
            *[pltpu.VMEM(x.shape, x.dtype) for x in (*windows, key_one, value_one, key_two, value_two)],
            pltpu.SemaphoreType.DMA((10,)),
            pltpu.VMEM(long_one, jnp.float32),
            pltpu.VMEM(long_one, jnp.float32),
            pltpu.VMEM(long_two, jnp.float32),
            pltpu.VMEM(long_two, jnp.float32),
            pltpu.VMEM(long_two, jnp.float32),
            pltpu.VMEM((WIN_ONE, depth), jnp.bfloat16),
            pltpu.VMEM((WIN_ONE, 2 * depth), jnp.bfloat16),
            pltpu.VMEM((WIN_TWO * heads, WIN_ONE), jnp.float32),
        ],
    )(queries, *halos, key_one, value_one, key_two, value_two)


def solution(mesh):
    rows = P(("seq", "head"), None)
    placed = (P(("seq", "head"), None, None), rows, rows, rows, rows)
    return jax.shard_map(
        body, mesh=mesh, in_specs=placed, out_specs=P(("seq", "head"), None, None), check_vma=False
    )
```

```python
import functools
import math

import jax
import jax.numpy as jnp
from jax import lax
from jax.experimental import pallas as pl
from jax.experimental.pallas import tpu as pltpu
from jax.sharding import PartitionSpec as P

WIN_ONE = 512
WIN_TWO = 32
LAG_CHUNK = 8
ROW_L = 1
COL_L = 2
ROW_B = 4


def pieces_behind(window, rows):
    return (window - 2) // rows + 1


def shards_behind(reach, inner):
    return (reach + inner - 1) // inner


def halo_kernel(reach, k1, v1, k2, v2, k1_out, v1_out, k2_out, v2_out, *sems):
    side_send, side_recv, fore_send, fore_recv, near_send, near_recv = sems
    inner, outer = lax.axis_size("head"), lax.axis_size("seq")
    seq, col = lax.axis_index("seq"), lax.axis_index("head")
    me, count = seq * inner + col, outer * inner
    shards = shards_behind(reach[0], inner)
    base = shards * inner
    firsts = ((k1, k1_out), (v1, v1_out))
    seconds = ((k2, k2_out), (v2, v2_out))

    def remote(source, target, send, recv, where):
        return pltpu.make_async_remote_copy(
            src_ref=source,
            dst_ref=target,
            send_sem=send,
            recv_sem=recv,
            device_id=where,
            device_id_type=pl.DeviceIdType.MESH,
        )

    def around(turn):
        return (col + turn) % inner

    def side(turn):
        return [
            remote(
                source,
                target.at[base + col],
                side_send.at[flow, turn - 1],
                side_recv.at[flow, turn - 1],
                (seq, around(turn)),
            )
            for flow, (source, target) in enumerate(firsts)
        ]

    def side_arrival(turn):
        return [
            remote(
                source,
                target.at[base + around(turn)],
                side_send.at[flow, inner - turn - 1],
                side_recv.at[flow, inner - turn - 1],
                (seq, around(turn)),
            )
            for flow, (source, target) in enumerate(firsts)
        ]

    def fore(hop, turn):
        return [
            remote(
                source if turn == 0 else target.at[base + around(turn)],
                target.at[(shards - hop) * inner + around(turn)],
                fore_send.at[flow, hop - 1, turn],
                fore_recv.at[flow, hop - 1, turn],
                (seq + hop, col),
            )
            for flow, (source, target) in enumerate(firsts)
        ]

    def near(step):
        there = me + step
        return [
            remote(
                source,
                target.at[reach[1] - step],
                near_send.at[flow, step - 1],
                near_recv.at[flow, step - 1],
                (there // inner, there % inner),
            )
            for flow, (source, target) in enumerate(seconds)
        ]

    def wanted(hop, turn):
        return hop * inner <= reach[0] + around(turn) - col

    def greet(where):
        pl.semaphore_signal(barrier, inc=1, device_id=where, device_id_type=pl.DeviceIdType.MESH)

    barrier = pltpu.get_barrier_semaphore()
    hops = (reach[0] + inner - 1 - col) // inner
    for turn in range(1, inner):
        greet((seq, around(turn)))
    for hop in range(1, shards + 1):

        @pl.when((seq - hop >= 0) & (hop <= hops))
        def _():
            greet((seq - hop, col))

    for step in range(1, reach[1] + 1):

        @pl.when(me - step >= 0)
        def _():
            greet(((me - step) // inner, (me - step) % inner))

    peers = inner - 1 + jnp.minimum(hops, outer - 1 - seq) + jnp.minimum(reach[1], count - 1 - me)
    pl.semaphore_wait(barrier, peers)

    for turn in range(1, inner):
        for copy in side(turn):
            copy.start()
    for turn in range(inner):
        if turn:
            for copy in side_arrival(turn):
                copy.wait_recv()
        for hop in range(shards, 0, -1):

            @pl.when((seq + hop < outer) & wanted(hop, turn))
            def _():
                for copy in fore(hop, turn):
                    copy.start()

        if turn == 0:
            for step in range(1, reach[1] + 1):

                @pl.when(me + step < count)
                def _():
                    for copy in near(step):
                        copy.start()

    for turn in range(inner):
        for hop in range(shards, 0, -1):

            @pl.when((seq - hop >= 0) & wanted(hop, turn))
            def _():
                for copy in fore(hop, turn):
                    copy.wait_recv()

            @pl.when((seq + hop < outer) & wanted(hop, turn))
            def _():
                for copy in fore(hop, turn):
                    copy.wait_send()

    for step in range(1, reach[1] + 1):

        @pl.when(me - step >= 0)
        def _():
            for copy in near(step):
                copy.wait_recv()

        @pl.when(me + step < count)
        def _():
            for copy in near(step):
                copy.wait_send()

    for turn in range(1, inner):
        for copy in side(turn):
            copy.wait_send()


def attend_kernel(*refs):
    q_far, far, out, q, near, fetched = refs[0], refs[1:9], refs[9], refs[10], refs[11:19], refs[19]
    k1f, v1f, k2f, v2f, one2, kw, vw, scores = refs[20:]
    piece, heads, depth = q.shape
    inner = lax.axis_size("head")
    reach = near[0].shape[0]
    skip = lax.axis_index("head") + shards_behind(reach, inner) * inner - reach
    far = [far[0].at[pl.ds(skip, reach)], far[1].at[pl.ds(skip, reach)], *far[2:]]
    fetches = [
        pltpu.make_async_copy(source, target, fetched.at[index])
        for index, (source, target) in enumerate(zip(far, near))
    ]
    early = pltpu.make_async_copy(q_far.at[pl.ds(0, 1)], q.at[pl.ds(0, 1)], fetched.at[8])
    rest = pltpu.make_async_copy(q_far.at[pl.ds(1, piece - 1)], q.at[pl.ds(1, piece - 1)], fetched.at[9])
    for fetch in fetches:
        fetch.start()
    early.start()
    rest.start()
    k1h, v1h, k2h, v2h, k1, v1, k2, v2 = near
    for fetch in fetches:
        fetch.wait()
    inner = lax.axis_size("head")
    me = lax.axis_index("seq") * inner + lax.axis_index("head")
    lead_one = k1h.shape[0] * piece
    lead_two = k2h.shape[0] * piece
    scale = 1.0 / math.sqrt(depth)

    def spread(target, behind, own):
        for slot in range(behind.shape[0]):
            target[slot * piece : (slot + 1) * piece, :] = behind[slot].astype(jnp.float32)
        lead = behind.shape[0] * piece
        target[lead : lead + piece, :] = own[...].astype(jnp.float32)

    spread(k1f, k1h, k1)
    spread(v1f, v1h, v1)
    spread(k2f, k2h, k2)
    spread(v2f, v2h, v2)
    first_one = lead_one - me * piece
    first_two = lead_two - me * piece

    @pl.when(first_one > 0)
    def _():
        pos = lax.broadcasted_iota(jnp.int32, k1f.shape, 0)
        whole = k1f[...]
        head_row = jnp.sum(jnp.where(pos == first_one, whole, 0.0), axis=0, keepdims=True)
        k1f[...] = jnp.where(pos < first_one, head_row, whole)
        v1f[...] = jnp.where(pos < first_one, 0.0, v1f[...])

    pos_two = lax.broadcasted_iota(jnp.int32, k2f.shape, 0)
    whole_two = k2f[...]
    head_two = jnp.sum(jnp.where(pos_two == first_two, whole_two, 0.0), axis=0, keepdims=True)
    k2f[...] = jnp.where(pos_two < first_two, head_two, whole_two) * scale
    v2f[...] = jnp.where(pos_two < first_two, 0.0, v2f[...])
    one2[...] = jnp.where(pos_two < first_two, 0.0, 1.0)

    span = LAG_CHUNK * heads
    lane_pos = lax.broadcasted_iota(jnp.int32, (WIN_ONE, depth), 0)

    def load_keys(token, slot):
        kw[slot] = k1f[pl.ds(lead_one + token - (WIN_ONE - 1), WIN_ONE), :].astype(jnp.bfloat16)

    def logits(token, chunk, top, slot):
        query = q[token].astype(jnp.float32)
        rows = []
        for lag in range(chunk * LAG_CHUNK, (chunk + 1) * LAG_CHUNK):
            near = k2f[pl.ds(lead_two + token - lag, 1), :]
            rows.append((query * near).astype(jnp.bfloat16))
        product = jnp.concatenate(rows, axis=0)
        for lo in range(0, span, span // ROW_L):
            for col in range(0, WIN_ONE, WIN_ONE // COL_L):
                made = lax.dot_general(
                    product[lo : lo + span // ROW_L],
                    kw[slot, col : col + WIN_ONE // COL_L, :],
                    (((1,), (1,)), ((), ())),
                    preferred_element_type=jnp.float32,
                )
                scores[chunk * span + lo : chunk * span + lo + span // ROW_L, col : col + WIN_ONE // COL_L] = made
                best = jnp.max(made.reshape(LAG_CHUNK // ROW_L, heads, WIN_ONE // COL_L), axis=0)
                for lane in range(0, WIN_ONE // COL_L, depth):
                    part = best[:, lane : lane + depth]
                    top = part if top is None else jnp.maximum(top, part)
        return top

    chunks = WIN_TWO // LAG_CHUNK
    load_keys(0, 0)
    early.wait()
    start_top = None
    for chunk in range(chunks):
        start_top = logits(0, chunk, start_top, 0)

    def step(token, top, slot):
        start = lead_one + token - (WIN_ONE - 1)
        vw[slot, :, :depth] = v1f[pl.ds(start, WIN_ONE), :].astype(jnp.bfloat16)
        vw[slot, :, depth:] = jnp.where(lane_pos + start < first_one, 0.0, 1.0).astype(jnp.bfloat16)
        later = jnp.minimum(token + 1, piece - 1)
        load_keys(later, 1 - slot)
        peak = jnp.max(top, axis=1, keepdims=True)
        num = den = later_top = None
        def weigh(chunk):
            base = chunk * span
            parts = scores[base : base + span, :].reshape(LAG_CHUNK, heads, WIN_ONE)
            return jnp.exp(parts - peak[None]).astype(jnp.bfloat16)

        def blend(chunk, raised, num, den):
            sub = LAG_CHUNK // ROW_B
            for lo in range(0, LAG_CHUNK, sub):
                mixed = jnp.dot(
                    raised[lo : lo + sub].reshape(sub * heads, WIN_ONE),
                    vw[slot],
                    preferred_element_type=jnp.float32,
                )
                mixed = mixed.reshape(sub, heads, 2 * depth)
                for index in range(sub):
                    row = lead_two + token - (chunk * LAG_CHUNK + lo + index)
                    more = mixed[index, :, :depth] * v2f[pl.ds(row, 1), :]
                    count = mixed[index, :, depth:] * one2[pl.ds(row, 1), :]
                    num = more if num is None else num + more
                    den = count if den is None else den + count
            return num, den

        for chunk in range(chunks):
            raised = weigh(chunk)
            if chunk + 1 < chunks:
                num, den = blend(chunk, raised, num, den)
                later_top = logits(later, chunk, later_top, 1 - slot)
            else:
                later_top = logits(later, chunk, later_top, 1 - slot)
                num, den = blend(chunk, raised, num, den)
        out[token] = (num / den).astype(out.dtype)
        return later_top

    rest.wait()
    unroll = math.gcd(piece, 2)

    def several(index, top):
        for turn in range(unroll):
            top = step(index * unroll + turn, top, turn % 2 if unroll > 1 else 0)
        return top

    lax.fori_loop(0, piece // unroll, several, start_top)


def body(queries, key_one, value_one, key_two, value_two):
    piece, heads, depth = queries.shape
    reach = (pieces_behind(WIN_ONE, piece), pieces_behind(WIN_TWO, piece))
    anywhere = pl.BlockSpec(memory_space=pl.ANY)
    vmem = pl.BlockSpec(memory_space=pltpu.VMEM)
    inner = lax.axis_size("head")
    shards = shards_behind(reach[0], inner)
    slots = (shards + 1) * inner
    behind = [jax.ShapeDtypeStruct((r, piece, depth), key_one.dtype) for r in (slots, slots, reach[1], reach[1])]
    windows = [jax.ShapeDtypeStruct((r, piece, depth), key_one.dtype) for r in (reach[0], reach[0], reach[1], reach[1])]
    halos = pl.pallas_call(
        functools.partial(halo_kernel, reach),
        out_shape=behind,
        in_specs=[anywhere] * 4,
        out_specs=[anywhere] * 4,
        scratch_shapes=[
            *[pltpu.SemaphoreType.DMA((2, inner))] * 2,
            *[pltpu.SemaphoreType.DMA((2, shards, inner))] * 2,
            *[pltpu.SemaphoreType.DMA((2, reach[1]))] * 2,
        ],
        compiler_params=pltpu.CompilerParams(collective_id=0, has_side_effects=True),
    )(key_one, value_one, key_two, value_two)
    long_one = ((reach[0] + 1) * piece, depth)
    long_two = ((reach[1] + 1) * piece, depth)
    return pl.pallas_call(
        attend_kernel,
        out_shape=jax.ShapeDtypeStruct(queries.shape, queries.dtype),
        in_specs=[anywhere] * 9,
        out_specs=vmem,
        scratch_shapes=[
            pltpu.VMEM(queries.shape, queries.dtype),
            *[pltpu.VMEM(x.shape, x.dtype) for x in (*windows, key_one, value_one, key_two, value_two)],
            pltpu.SemaphoreType.DMA((10,)),
            pltpu.VMEM(long_one, jnp.float32),
            pltpu.VMEM(long_one, jnp.float32),
            pltpu.VMEM(long_two, jnp.float32),
            pltpu.VMEM(long_two, jnp.float32),
            pltpu.VMEM(long_two, jnp.float32),
            pltpu.VMEM((2, WIN_ONE, depth), jnp.bfloat16),
            pltpu.VMEM((2, WIN_ONE, 2 * depth), jnp.bfloat16),
            pltpu.VMEM((WIN_TWO * heads, WIN_ONE), jnp.float32),
        ],
    )(queries, *halos, key_one, value_one, key_two, value_two)


def solution(mesh):
    rows = P(("seq", "head"), None)
    placed = (P(("seq", "head"), None, None), rows, rows, rows, rows)
    return jax.shard_map(
        body, mesh=mesh, in_specs=placed, out_specs=P(("seq", "head"), None, None), check_vma=False
    )
```
